512 devices in a mesh: sub: 128 (over y, z, core), grp: 4 (over x).
Axes of the slice: x: 4, y: 8, z: 8, core: 2. Of those that a mesh axis runs over, the one named last changes fastest.
Arguments:
- lam_start: float32 [524288, 128], P(('sub', 'grp')), may hold values from -6 to 6
- loads: float32 [524288, 128], P(('sub', 'grp')), may hold values from -40 to 40
- dual_ops: bfloat16 [512, 1024, 1024], P(('sub', 'grp')), may hold values from -40 to 40, as said below
- modes: float32 [6, 524288], P(None, ('sub', 'grp')), may hold values from -0.6 to 0.6
- coarse_inverse: float32 [3072, 3072], P('sub', 'grp'), may hold values from -1 to 1, as said below
- face_offset: int32 [128, 4, 8], P(None, 'grp'), may hold values from 0 to 3, as said below
- face_block: int32 [128, 4, 8], P(None, 'grp'), may hold values from 0 to 7
- face_sign: int32 [128, 4, 8], P(None, 'grp'), may hold values from 0 to 1
- contact: int32 [3, 524288], P(None, ('sub', 'grp')), may hold values 0 or 1
Outputs:
- multipliers: float32 [524288, 128], P(('sub', 'grp'))
The draws below stay inside these ranges and needn't reach their ends.
Inputs may be any that keep to these rules, and one draw needn't show every extreme that they name: Each block dual_ops[k] is symmetric positive definite. coarse_inverse is symmetric positive definite. `face_offset`: no face reads from outside the order 0 to 127. For every subdomain no value is taken by more than 4 of its faces, and exactly 4 of its faces share one value.
All inputs are finite; a program needn't handle non-finite values. No bound on the sum of `contact` on one device may be relied on, other than what follows from the above.
Results may differ from the reference program's by a relative error of at most 0.005.
Values may be sent and summed in bfloat16 or wider, within the bound.
A program may use at most 64 MiB of HBM per device.

```python
import math
import jax
import jax.numpy as jnp
from jax import lax

ORDER = 1024
FACES = 8
FACE_ROWS = 32
CAP = 4
MODES = 6
STEPS = 3
LOADS = 128
SUBS = 512
ROWS = 524288
COARSE_ORDER_SIZE = 3072
N_SUB = 128
N_GRP = 4


def draw_dual_ops(key, part):
    keys = jax.random.split(jax.random.fold_in(key, 11), SUBS)

    def one_block(sub_key):
        key_a, key_b = jax.random.split(sub_key, 2)
        base = jax.random.normal(key_a, (ORDER, ORDER), jnp.float32)
        sym = (base + base.T) * (0.7 / math.sqrt(2.0 * ORDER))
        diag = jax.random.uniform(key_b, (ORDER,), jnp.float32, 2.0, 4.0)
        matrix = sym + jnp.diag(diag)
        return matrix.astype(jnp.bfloat16)
    return lax.map(one_block, keys)


def draw_coarse_inverse(key, part):
    key_a, key_b, key_c = jax.random.split(jax.random.fold_in(key, 23), 3)
    half = COARSE_ORDER_SIZE // 2
    base = jax.random.normal(key_a, (COARSE_ORDER_SIZE, COARSE_ORDER_SIZE), jnp.float32)
    sym = (base + base.T) * (0.1 / math.sqrt(2.0 * COARSE_ORDER_SIZE))
    diag = jax.random.uniform(key_b, (COARSE_ORDER_SIZE,), jnp.float32, 0.7, 1.3)
    pair_weight = jax.random.uniform(key_c, (half,), jnp.float32, 0.15, 0.3)
    row_ids = jnp.arange(COARSE_ORDER_SIZE, dtype=jnp.int32)
    pair_row = jnp.concatenate([pair_weight, pair_weight])
    partner = (row_ids + half) % COARSE_ORDER_SIZE
    coupling = jnp.where(partner[:, None] == row_ids[None, :], pair_row[:, None], 0.0)
    return (sym + jnp.diag(diag) + coupling) * (100.0 / ORDER)


def draw_loads(key, part):
    key_a = jax.random.fold_in(jax.random.fold_in(key, 37), 0)
    base = jax.random.normal(key_a, (ROWS, LOADS), jnp.float32)
    sub_pos = (jnp.arange(ROWS) // (ORDER * N_GRP)).astype(jnp.float32)
    rise = jnp.exp(math.log(3.0) * sub_pos / max(N_SUB - 1, 1))
    values = base * rise[:, None]
    return jnp.clip(values, -40.0, 40.0)


def draw_face_offset(key, part):
    key_a, key_b, key_c = jax.random.split(jax.random.fold_in(key, 51), 3)
    steps_tab = jnp.array([-2, -1, 1, 2], jnp.int32)
    sub_pos = jnp.arange(N_SUB, dtype=jnp.int32)[:, None, None]
    target = sub_pos + steps_tab[None, None, :]
    valid = (target >= 0) & (target < N_SUB)
    four = jnp.arange(4, dtype=jnp.int32)
    score = jax.random.randint(key_a, (N_SUB, N_GRP, 4), 0, 1 << 20) * 4 + four
    score = jnp.where(valid, score, -1)
    main = jnp.argmax(score, axis=-1).astype(jnp.int32)
    score_rest = jax.random.randint(key_b, (N_SUB, N_GRP, FACES - CAP, 4), 0, 1 << 20) * 4 + four
    allowed = valid[:, :, None, :] & (four[None, None, None, :] != main[:, :, None, None])
    score_rest = jnp.where(allowed, score_rest, -1)
    rest = jnp.argmax(score_rest, axis=-1).astype(jnp.int32)
    labels = jnp.concatenate([jnp.broadcast_to(main[:, :, None], (N_SUB, N_GRP, CAP)), rest], axis=-1)
    order_key = jax.random.randint(key_c, (N_SUB, N_GRP, FACES), 0, 1 << 20) * FACES + jnp.arange(FACES, dtype=jnp.int32)
    perm = jnp.argsort(order_key, axis=-1)
    return jnp.take_along_axis(labels, perm, axis=-1).astype(jnp.int32)


def place_ends(values, key, least, high):
    longest = values.shape.index(max(values.shape))
    spots = []
    for shift in (0, 1):
        where = [jax.random.randint(jax.random.fold_in(key, axis), (), 0, length) for axis, length in enumerate(values.shape)]
        where[longest] = (where[longest] + shift) % values.shape[longest]
        spots.append(tuple(where))
    return values.at[spots[0]].set(least).at[spots[1]].set(high)


def levels(key, shape, shards, smallest, high):
    def one(position, shards_of):
        heights = jax.random.uniform(jax.random.fold_in(jax.random.fold_in(key, 6), position), (shards_of,), jnp.float32, smallest / len(shards), high / len(shards))
        return jnp.repeat(jnp.exp(heights), shape[position] // shards_of).reshape((-1,) + (1,) * (len(shape) - position - 1))

    loudness = one(*shards[0])
    for cut in shards[1:]:
        loudness = loudness * one(*cut)
    return loudness


def scatter_about(stream_key, dims, spread, bound, shards=(), kind=jnp.bfloat16):
    values = jax.random.normal(stream_key, dims, jnp.float32) * spread
    if len(shards) > 0:
        values = levels(stream_key, dims, shards, -0.22, 0.18) * values
    return jnp.clip(values, min=-bound, max=bound).astype(kind)


def setup_inputs(seed: int = 0) -> dict:
    streams_of = jax.random.split(jax.random.key(seed), 10)
    return {
        "lam_start": scatter_about(streams_of[0], (ROWS, LOADS), 1.0, 6.0, ((0, 512),), jnp.float32),
        "loads": draw_loads(jax.random.fold_in(streams_of[9], 71), 0),
        "dual_ops": draw_dual_ops(jax.random.fold_in(streams_of[9], 71), 0),
        "modes": scatter_about(streams_of[3], (MODES, ROWS), 0.1, 0.6, ((1, 512),), jnp.float32),
        "coarse_inverse": draw_coarse_inverse(jax.random.fold_in(streams_of[9], 71), 0),
        "face_offset": draw_face_offset(jax.random.fold_in(streams_of[9], 71), 0),
        "face_block": place_ends(jax.random.randint(streams_of[6], (N_SUB, N_GRP, FACES), 0, FACES), jax.random.fold_in(streams_of[6], 1), 0, FACES - 1).astype(jnp.int32),
        "face_sign": place_ends(jax.random.randint(streams_of[7], (N_SUB, N_GRP, FACES), 0, 2), jax.random.fold_in(streams_of[7], 1), 0, 1).astype(jnp.int32),
        "contact": place_ends((jax.random.randint(streams_of[8], (STEPS, ROWS), 0, 4) < 1).astype(jnp.int32), jax.random.fold_in(streams_of[8], 1), 0, 1),
    }


def neighbour_maps(face_offset, face_block, face_sign):
    steps_tab = jnp.array([-2, -1, 1, 2], jnp.int32)
    moved = steps_tab[face_offset]
    sub_pos = jnp.arange(N_SUB, dtype=jnp.int32)[:, None, None]
    grp_pos = jnp.arange(N_GRP, dtype=jnp.int32)[None, :, None]
    target = ((sub_pos + moved) * N_GRP + grp_pos).reshape(SUBS, FACES).astype(jnp.int32)
    blocks = face_block.reshape(SUBS, FACES).astype(jnp.int32)
    signs = (2 * face_sign - 1).astype(jnp.float32).reshape(SUBS, FACES)
    return target, blocks, signs


def apply_dual(field, dual_ops, target, blocks, signs):
    normal_loads = field.shape[-1]
    face_total = FACES * FACE_ROWS
    low = field.astype(jnp.bfloat16)
    faces = low[:, :face_total].reshape(SUBS, FACES, FACE_ROWS, normal_loads)
    remote = faces[target, blocks]
    zfaces = (faces.astype(jnp.float32) + signs[:, :, None, None] * remote.astype(jnp.float32)).astype(jnp.bfloat16)
    zfull = jnp.concatenate([zfaces.reshape(SUBS, face_total, normal_loads), low[:, face_total:]], axis=1)

    def one_block(pair):
        return jnp.dot(pair[0].astype(jnp.float32), pair[1].astype(jnp.float32), precision=lax.Precision.HIGHEST)

    image = lax.map(one_block, (dual_ops, zfull)).astype(jnp.bfloat16)
    yfaces = image[:, :face_total].reshape(SUBS, FACES, FACE_ROWS, normal_loads).astype(jnp.float32)
    returned = jnp.zeros((SUBS, FACES, FACE_ROWS, normal_loads), jnp.float32).at[target, blocks].add(signs[:, :, None, None] * yfaces)
    result = image.astype(jnp.float32)
    return result.at[:, :face_total].add(returned.reshape(SUBS, face_total, normal_loads))


def reference(lam_start, loads, dual_ops, modes, coarse_inverse, face_offset, face_block, face_sign, contact):
    target, blocks, signs = neighbour_maps(face_offset, face_block, face_sign)
    normal_loads = lam_start.shape[-1]
    lam = lam_start.reshape(SUBS, ORDER, normal_loads)
    rhs = loads.reshape(SUBS, ORDER, normal_loads)
    coarse_basis_columns = modes.reshape(MODES, SUBS, ORDER)
    for step in range(STEPS):
        dual_gradient = apply_dual(lam, dual_ops, target, blocks, signs) - rhs
        coarse_residual_part = jnp.einsum('vfj,fjy->fvy', coarse_basis_columns, dual_gradient, precision=lax.Precision.HIGHEST).reshape(COARSE_ORDER_SIZE, normal_loads)
        correction_term = jnp.dot(coarse_inverse, coarse_residual_part, precision=lax.Precision.HIGHEST).reshape(SUBS, MODES, normal_loads)
        search_direction = dual_gradient - jnp.einsum('goc,ogh->och', coarse_basis_columns, correction_term, precision=lax.Precision.HIGHEST)
        image = apply_dual(search_direction, dual_ops, target, blocks, signs)
        slope = jnp.sum(dual_gradient * search_direction, axis=(0, 1))
        curv = jnp.sum(search_direction * image, axis=(0, 1))
        alpha = slope / curv
        lam = lam - alpha[None, None, :] * search_direction
        active = contact[step].reshape(SUBS, ORDER)[:, :, None] == 1
        lam = jnp.where(active, jnp.maximum(lam, 0.0), lam)
    return lam.reshape(ROWS, normal_loads)
```

```python
import jax
import jax.numpy as jnp
from jax import lax
from jax.experimental import pallas as pl
from jax.experimental.pallas import tpu as pltpu
from jax.sharding import PartitionSpec as P

MESH = pl.DeviceIdType.MESH
FACES = 8
FACE_ROWS = 32
FACE_TOTAL = FACES * FACE_ROWS
CAP = 4
SLOTS = 4 * CAP
MODES = 6
STEPS = 3
MOVES = (-2, -1, 1, 2)
NY, NL, NX = 8, 16, 4
NXY = NY * NX
ORDER = 1024
LOADS = 128
F32, BF16 = jnp.float32, jnp.bfloat16
LOW = -3.0e38


def dot(a, b):
    return jnp.dot(a, b, preferred_element_type=F32)


def dot_t(a, b):
    return lax.dot_general(a, b, (((0,), (0,)), ((), ())), preferred_element_type=F32)


def parts_of(x, count):
    parts = []
    for _ in range(count):
        part = x.astype(BF16).astype(F32)
        parts.append(part)
        x = x - part
    return parts


def wait_bytes(sem, ref):
    pltpu.make_async_copy(ref, ref, sem).wait()


def kernel(face_offset, face_block, face_sign, lam_in, loads, dual, modes, cinv, contact, out, *scratch):
    (place, leave, pick, vz, ybf, zf, grad, dirn, modes_rows, modes_cols, floor, spread, fsend, bsend, eline, part, cpl, arl, arp,
     csend, cmat, cpad, fs, fr, bs, br, es, er, cs, cr, als, alr, aps, apr, ks, kr) = scratch[:36]
    farr = scratch[36:42]
    barr = scratch[42:45]
    s = lax.axis_index("sub")
    x = lax.axis_index("grp")
    n_sub = NY * NL
    y = s // NL
    l = s % NL
    me = y * NX + x

    barrier = pltpu.get_barrier_semaphore()

    def line_dev(i):
        return (y * NL + (l + i) % NL, x)

    def plane_idx(i):
        return (me + i) % NXY

    def plane_dev(q):
        return ((q // NX) * NL + l, q % NX)

    def around(move):
        return ((s + move + n_sub) % n_sub, x)

    def greet(device):
        pl.semaphore_signal(barrier, 1, device_id=device, device_id_type=MESH)

    def greet_line(i, carry):
        greet(line_dev(i))
        return carry

    def greet_plane(i, carry):
        greet(plane_dev(plane_idx(i)))
        return carry

    for move in MOVES:
        greet(around(move))
    lax.fori_loop(1, NL, greet_line, 0)
    lax.fori_loop(1, NXY, greet_plane, 0)

    def remote(src, dst, ssem, rsem, device):
        pltpu.make_async_remote_copy(
            src_ref=src, dst_ref=dst, send_sem=ssem, recv_sem=rsem, device_id=device, device_id_type=MESH
        ).start()

    def same_row(rows, cols):
        row = lax.broadcasted_iota(jnp.int32, (rows, cols), 0)
        col = lax.broadcasted_iota(jnp.int32, (rows, cols), 1)
        return jnp.where(row % FACE_ROWS == col % FACE_ROWS, col // FACE_ROWS, -1)

    wide = same_row(FACE_ROWS, SLOTS * FACE_ROWS)
    narrow = same_row(FACE_ROWS, FACE_TOTAL)
    own_off = [face_offset[f, s] for f in range(FACES)]
    own_slot = []
    for f in range(FACES):
        rank = jnp.int32(0)
        for g in range(f):
            rank = rank + jnp.where(own_off[g] == own_off[f], 1, 0)
        own_slot.append(own_off[f] * CAP + rank)
        sign = (2 * face_sign[f, s] - 1).astype(F32)
        place[f * FACE_ROWS : (f + 1) * FACE_ROWS, :] = jnp.where(wide == own_slot[f], sign, 0.0).astype(BF16)
    for q in range(SLOTS):
        face = jnp.int32(0)
        for f in range(FACES):
            face = face + jnp.where(own_slot[f] == q, f, 0)
        leave[q * FACE_ROWS : (q + 1) * FACE_ROWS, :] = jnp.where(narrow == face, 1.0, 0.0).astype(BF16)
    lane = lax.broadcasted_iota(jnp.int32, (1, SLOTS * FACE_ROWS), 1)
    block_of = jnp.full((1, SLOTS * FACE_ROWS), -1, jnp.int32)
    sign_of = jnp.zeros((1, SLOTS * FACE_ROWS), F32)
    for w, move in enumerate(MOVES):
        reader = (s - move + n_sub) % n_sub
        far_off = [face_offset[f, reader] for f in range(FACES)]
        far_block = [face_block[f, reader] for f in range(FACES)]
        far_sign = [2 * face_sign[f, reader] - 1 for f in range(FACES)]
        count = jnp.int32(0)
        slot_of = []
        for f in range(FACES):
            hit = far_off[f] == w
            slot_of.append(jnp.where(hit, count, -1))
            count = count + jnp.where(hit, 1, 0)
        for j in range(CAP):
            q = w * CAP + j
            block = jnp.int32(0)
            sign = jnp.int32(0)
            for f in range(FACES):
                hit = slot_of[f] == j
                block = block + jnp.where(hit, far_block[f], 0)
                sign = sign + jnp.where(hit, far_sign[f], 0)
            pick[q * FACE_ROWS : (q + 1) * FACE_ROWS, :] = jnp.where(narrow == block, 1.0, 0.0).astype(BF16)
            inside = lane // FACE_ROWS == q
            block_of = jnp.where(inside, block, block_of)
            sign_of = jnp.where(inside, sign.astype(F32), sign_of)
    for b in range(FACES):
        hit = (wide >= 0) & (block_of == b)
        spread[b * FACE_ROWS : (b + 1) * FACE_ROWS, :] = jnp.where(hit, sign_of, 0.0).astype(BF16)

    def pack_and_send(n):
        packed = dot(pick[...], vz[0:FACE_TOTAL, :]).astype(BF16)
        fsend[n] = packed.reshape(SLOTS, FACE_ROWS, LOADS)
        for w, move in enumerate(MOVES):
            span = pl.ds(w * CAP, CAP)
            remote(fsend.at[n, span], farr[n].at[span], fs.at[n], fr.at[n], around(-move))

    out[...] = lam_in[...]
    vz[...] = lam_in[...].astype(BF16)

    pl.semaphore_wait(barrier, len(MOVES) + NL - 1 + NXY - 1)
    pack_and_send(0)

    cpad[...] = jnp.zeros(cpad.shape, F32)
    for b in range(NX):
        cpad[b * 8 : b * 8 + MODES, :] = cinv[b * MODES : (b + 1) * MODES, :]
    half = cinv.shape[1] // 2
    pick_r = lax.broadcasted_iota(jnp.int32, (half, LOADS), 0)
    pick_c = lax.broadcasted_iota(jnp.int32, (half, LOADS), 1)
    stack = jnp.concatenate(parts_of(cpad[...], 3), axis=0).astype(BF16)
    for xd in range(NX):
        want = ((pick_c // 8) * NX + xd) * MODES + pick_c % 8
        choose = jnp.where((pick_r == want) & (pick_c % 8 < MODES), 1.0, 0.0).astype(BF16)
        for h in range(2):
            got = dot(stack[:, h * half : (h + 1) * half], choose)
            csend[xd * 2 + h] = got[0:32] + got[32:64] + got[64:96]
    for xd in range(NX):
        for h in range(2):
            yd = 2 * x + h
            mine = (yd == y) & (x == xd)

            @pl.when(mine)
            def _():
                pltpu.make_async_copy(csend.at[xd * 2 + h], cmat.at[y], kr).start()

            @pl.when(jnp.logical_not(mine))
            def _():
                remote(csend.at[xd * 2 + h], cmat.at[y], ks, kr, (yd * NL + l, xd))

    m_pad = jnp.concatenate([modes[...], jnp.zeros((2, ORDER), F32)], axis=0)
    m_hi, m_lo = parts_of(m_pad, 2)
    modes_rows[...] = jnp.concatenate([m_hi, m_lo], axis=0).astype(BF16)
    m_all = jnp.concatenate([m_hi, m_hi, m_lo, jnp.zeros((8, ORDER), F32)], axis=0).astype(BF16)
    eye = (lax.broadcasted_iota(jnp.int32, (32, 32), 0) == lax.broadcasted_iota(jnp.int32, (32, 32), 1))
    modes_cols[...] = dot_t(m_all, eye.astype(F32).astype(BF16)).astype(BF16)
    con = jnp.concatenate([contact[...].astype(F32), jnp.zeros((16 - STEPS, ORDER), F32)], axis=0).astype(BF16)
    for t in range(STEPS):
        pick_t = (lax.broadcasted_iota(jnp.int32, (16, LOADS), 0) == t).astype(F32).astype(BF16)
        floor[t] = jnp.where(dot_t(con, pick_t) > 0.5, 0.0, LOW)

    def receive_faces(n, keep):
        wait_bytes(fr.at[n], farr[n])
        came = dot(place[...], farr[n][...].reshape(SLOTS * FACE_ROWS, LOADS))
        z = vz[0:FACE_TOTAL, :].astype(F32) + came
        if keep:
            zf[...] = z
        vz[0:FACE_TOTAL, :] = z.astype(BF16)

    def residual(rows_from, rows_to):
        g_hi, g_lo = parts_of(grad[rows_from:rows_to, :], 2)
        m = modes_rows[:, rows_from:rows_to]
        a = dot(m, g_hi.astype(BF16))
        b = dot(m, g_lo.astype(BF16))
        return a[0:8] + a[8:16] + b[0:8]

    for t in range(STEPS):
        if t > 0:
            vz[...] = out[...].astype(BF16)
            pack_and_send(2 * t)
        receive_faces(2 * t, False)
        ybf[...] = dot(dual[0, 0:FACE_TOTAL, :], vz[...]).astype(BF16)
        bsend[t] = dot(leave[...], ybf[...]).astype(BF16).reshape(SLOTS, FACE_ROWS, LOADS)
        for w, move in enumerate(MOVES):
            span = pl.ds(w * CAP, CAP)
            remote(bsend.at[t, span], barr[t].at[span], bs.at[t], br.at[t], around(move))
        y_rest = dot(dual[0, FACE_TOTAL:, :], vz[...]).astype(BF16).astype(F32)
        grad[FACE_TOTAL:, :] = y_rest - loads[FACE_TOTAL:, :]
        e_rest = residual(FACE_TOTAL, ORDER)
        wait_bytes(br.at[t], barr[t])
        back = dot(spread[...], barr[t][...].reshape(SLOTS * FACE_ROWS, LOADS))
        grad[0:FACE_TOTAL, :] = ybf[...].astype(F32) + back - loads[0:FACE_TOTAL, :]
        eline[t, l] = e_rest + residual(0, FACE_TOTAL)

        def send_e(i, carry):
            remote(eline.at[t, l], eline.at[t, l], es.at[t], er.at[t], line_dev(i))
            return carry

        lax.fori_loop(1, NL, send_e, 0)
        if t == 0:
            wait_bytes(kr, cmat)
        wait_bytes(er.at[t], eline.at[t, pl.ds(0, NL - 1)])
        product = jnp.dot(
            cmat[...].reshape(NXY * 8, LOADS), eline[t].reshape(NL * 8, LOADS),
            precision=lax.Precision.HIGHEST, preferred_element_type=F32,
        )
        part[t] = product.reshape(NXY, 8, LOADS)
        cpl[t, me] = part[t, me]

        def send_c(i, carry):
            q = plane_idx(i)
            remote(part.at[t, q], cpl.at[t, me], cs.at[t], cr.at[t], plane_dev(q))
            return carry

        lax.fori_loop(1, NXY, send_c, 0)
        wait_bytes(cr.at[t], cpl.at[t, pl.ds(0, NXY - 1)])
        c_hi, c_lo = parts_of(jnp.sum(cpl[t], axis=0), 2)
        c_all = jnp.concatenate([c_hi, c_lo, c_hi, jnp.zeros((8, LOADS), F32)], axis=0).astype(BF16)
        direction = grad[...] - dot(modes_cols[...], c_all)
        dirn[...] = direction
        vz[...] = direction.astype(BF16)
        pack_and_send(2 * t + 1)
        slope = jnp.sum(grad[...] * direction, axis=0, keepdims=True)

        receive_faces(2 * t + 1, True)
        image = dot(dual[0], vz[...]).astype(BF16).astype(F32)
        curv = jnp.sum(zf[...] * image[0:FACE_TOTAL], axis=0, keepdims=True)
        curv = curv + jnp.sum(dirn[FACE_TOTAL:, :] * image[FACE_TOTAL:], axis=0, keepdims=True)
        arl[t, l] = jnp.concatenate([slope, curv], axis=0)

        def send_line(i, carry):
            remote(arl.at[t, l], arl.at[t, l], als.at[t], alr.at[t], line_dev(i))
            return carry

        lax.fori_loop(1, NL, send_line, 0)
        wait_bytes(alr.at[t], arl.at[t, pl.ds(0, NL - 1)])
        arp[t, me] = jnp.sum(arl[t], axis=0)

        def send_plane(i, carry):
            remote(arp.at[t, me], arp.at[t, me], aps.at[t], apr.at[t], plane_dev(plane_idx(i)))
            return carry

        lax.fori_loop(1, NXY, send_plane, 0)
        wait_bytes(apr.at[t], arp.at[t, pl.ds(0, NXY - 1)])
        total = jnp.sum(arp[t], axis=0)
        alpha = total[0:1] / total[1:2]
        out[...] = jnp.maximum(out[...] - alpha * dirn[...], floor[t])

    for t in range(STEPS):
        for n in (2 * t, 2 * t + 1):
            wait_bytes(fs.at[n], fsend.at[n])
        wait_bytes(bs.at[t], bsend.at[t])
        wait_bytes(es.at[t], eline.at[t, pl.ds(0, NL - 1)])
        wait_bytes(cs.at[t], part.at[t, pl.ds(0, NXY - 1)])
        wait_bytes(als.at[t], arl.at[t, pl.ds(0, NL - 1)])
        wait_bytes(aps.at[t], arp.at[t, pl.ds(0, NXY - 1)])
    own_cut = (x == y // 2)

    @pl.when(own_cut)
    def _():
        wait_bytes(ks, csend.at[pl.ds(0, 7)])

    @pl.when(jnp.logical_not(own_cut))
    def _():
        wait_bytes(ks, csend)


def on_device(lam_start, loads, dual_ops, modes, coarse_inverse, face_offset, face_block, face_sign, contact):
    tables = [face[:, 0, :].T for face in (face_offset, face_block, face_sign)]
    vmem = pl.BlockSpec(memory_space=pltpu.VMEM)
    smem = pl.BlockSpec(memory_space=pltpu.SMEM)
    dma = pltpu.SemaphoreType.DMA
    face_buf = pltpu.VMEM((SLOTS, FACE_ROWS, LOADS), BF16)
    return pl.pallas_call(
        kernel,
        name="dual_steps",
        out_shape=jax.ShapeDtypeStruct(lam_start.shape, F32),
        in_specs=[smem] * 3 + [vmem] * 6,
        out_specs=vmem,
        scratch_shapes=[
            pltpu.VMEM((FACE_TOTAL, SLOTS * FACE_ROWS), BF16),
            pltpu.VMEM((SLOTS * FACE_ROWS, FACE_TOTAL), BF16),
            pltpu.VMEM((SLOTS * FACE_ROWS, FACE_TOTAL), BF16),
            pltpu.VMEM((ORDER, LOADS), BF16),
            pltpu.VMEM((FACE_TOTAL, LOADS), BF16),
            pltpu.VMEM((FACE_TOTAL, LOADS), F32),
            pltpu.VMEM((ORDER, LOADS), F32),
            pltpu.VMEM((ORDER, LOADS), F32),
            pltpu.VMEM((16, ORDER), BF16),
            pltpu.VMEM((ORDER, 32), BF16),
            pltpu.VMEM((STEPS, ORDER, LOADS), F32),
            pltpu.VMEM((FACE_TOTAL, SLOTS * FACE_ROWS), BF16),
            pltpu.VMEM((2 * STEPS, SLOTS, FACE_ROWS, LOADS), BF16),
            pltpu.VMEM((STEPS, SLOTS, FACE_ROWS, LOADS), BF16),
            pltpu.VMEM((STEPS, NL, 8, LOADS), F32),
            pltpu.VMEM((STEPS, NXY, 8, LOADS), F32),
            pltpu.VMEM((STEPS, NXY, 8, LOADS), F32),
            pltpu.VMEM((STEPS, NL, 2, LOADS), F32),
            pltpu.VMEM((STEPS, NXY, 2, LOADS), F32),
            pltpu.VMEM((8, 32, LOADS), F32),
            pltpu.VMEM((8, 32, LOADS), F32),
            pltpu.VMEM((32, coarse_inverse.shape[1]), F32),
            dma((2 * STEPS,)),
            dma((2 * STEPS,)),
        ]
        + [dma((STEPS,))] * 10
        + [dma, dma]
        + [face_buf] * (3 * STEPS),
        compiler_params=pltpu.CompilerParams(collective_id=1, has_side_effects=True),
    )(*tables, lam_start, loads, dual_ops, modes, coarse_inverse, contact)


def solution(mesh):
    both = ("sub", "grp")
    placed = (
        P(both, None),
        P(both, None),
        P(both, None, None),
        P(None, both),
        P("sub", "grp"),
        P(None, "grp", None),
        P(None, "grp", None),
        P(None, "grp", None),
        P(None, both),
    )
    return jax.shard_map(on_device, mesh=mesh, in_specs=placed, out_specs=P(both, None), check_vma=False)
```

```python
import jax
import jax.numpy as jnp
from jax import lax
from jax.experimental import pallas as pl
from jax.experimental.pallas import tpu as pltpu
from jax.sharding import PartitionSpec as P

MESH = pl.DeviceIdType.MESH
FACES = 8
FACE_ROWS = 32
FACE_TOTAL = FACES * FACE_ROWS
CAP = 4
SLOTS = 4 * CAP
SLOT_ROWS = SLOTS * FACE_ROWS
MODES = 6
STEPS = 3
MOVES = (-2, -1, 1, 2)
NY, NL, NX = 8, 16, 4
N_SUB = NY * NL
NXY = NY * NX
ORDER = 1024
LOADS = 128
F32, BF16 = jnp.float32, jnp.bfloat16
LOW = -3.0e38
LAM_HI, LAM_LO, CONTACT, DIR_HI, DIR_LO, MESSAGES = 0, 1, 2, 3, 6, 8


def dot(a, b):
    return jnp.dot(a, b, preferred_element_type=F32)


def dot_t(a, b):
    return lax.dot_general(a, b, (((0,), (0,)), ((), ())), preferred_element_type=F32)


def parts_of(x, count):
    parts = []
    for _ in range(count):
        part = x.astype(BF16).astype(F32)
        parts.append(part)
        x = x - part
    return parts


def iota(shape, dim):
    return lax.broadcasted_iota(jnp.int32, shape, dim)


def ones_where(mask):
    return jnp.where(mask, 1.0, 0.0).astype(BF16)


def same_row(cols):
    row, col = iota((FACE_ROWS, cols), 0), iota((FACE_ROWS, cols), 1)
    return jnp.where(row == (col & (FACE_ROWS - 1)), col >> 5, -1)


def wait_bytes(sem, ref):
    pltpu.make_async_copy(ref, ref, sem).wait()


def ring(step, size):
    return min(step, size - step)


def wrapped(base, step, size):
    return jnp.where(base + step >= size, base + step - size, base + step)


def kernel(face_offset, face_block, face_sign, lam_hbm, loads_hbm, dual_hbm, modes_hbm, cinv_hbm, contact_hbm, out, *scratch):
    (loads, dual, modes, cinv, contact, place, leave, pick, spread, vz, low, ybf, zf, grad, dirn, image, lam_far, modes_rows,
     modes_cols, columns, floor, floor_far, fsend, farr, bsend, barr, eline, part, cpl, arl, arp, csend, cmat, cpad,
     load_sem, fs, fr, bs, br, es, er, cs, cr, als, alr, aps, apr, ks, kr) = scratch
    s = lax.axis_index("sub")
    x = lax.axis_index("grp")
    y = s // NL
    l = s % NL
    me = y * NX + x

    fetches = []
    for i, (src, dst) in enumerate(((lam_hbm, out), (modes_hbm, modes), (cinv_hbm, cinv), (contact_hbm, contact),
                                    (dual_hbm, dual), (loads_hbm, loads))):
        fetches.append(pltpu.make_async_copy(src, dst, load_sem.at[i]))
        fetches[i].start()

    line = [(y * NL + wrapped(l, i, NL), x) for i in sorted(range(1, NL), key=lambda i: -ring(i, NL))]
    ys = [y] + [wrapped(y, i, NY) for i in range(1, NY)]
    xs = [x] + [wrapped(x, i, NX) for i in range(1, NX)]
    steps = sorted(((i, j) for i in range(NY) for j in range(NX) if i + j > 0), key=lambda p: -ring(p[0], NY) - ring(p[1], NX))
    plane = [(ys[i] * NX + xs[j], (ys[i] * NL + l, xs[j])) for i, j in steps]
    around = {move: (wrapped(s, (move + N_SUB) % N_SUB, N_SUB), x) for move in MOVES}

    barrier = pltpu.get_barrier_semaphore()
    for device in [around[move] for move in MOVES] + line + [device for _, device in plane]:
        pl.semaphore_signal(barrier, 1, device_id=device, device_id_type=MESH)

    def remote(src, dst, ssem, rsem, device):
        pltpu.make_async_remote_copy(
            src_ref=src, dst_ref=dst, send_sem=ssem, recv_sem=rsem, device_id=device, device_id_type=MESH
        ).start()

    wide = same_row(SLOT_ROWS)
    narrow = same_row(FACE_TOTAL)
    lane_slot = iota((1, SLOT_ROWS), 1) >> 5
    block_of = jnp.full((1, SLOT_ROWS), -1, jnp.int32)
    sign_of = jnp.zeros((1, SLOT_ROWS), F32)
    for w, move in enumerate(MOVES):
        reader = around[-move][0]
        far_block = [face_block[f, reader] for f in range(FACES)]
        far_sign = [2 * face_sign[f, reader] - 1 for f in range(FACES)]
        count = jnp.int32(0)
        slot_of = []
        for f in range(FACES):
            hit = face_offset[f, reader] == w
            slot_of.append(jnp.where(hit, count, -1))
            count = count + jnp.where(hit, 1, 0)
        for j in range(CAP):
            q = w * CAP + j
            block = jnp.int32(0)
            sign = jnp.int32(0)
            for f in range(FACES):
                hit = slot_of[f] == j
                block = block + jnp.where(hit, far_block[f], 0)
                sign = sign + jnp.where(hit, far_sign[f], 0)
            pick[q * FACE_ROWS : (q + 1) * FACE_ROWS, :] = ones_where(narrow == block)
            block_of = jnp.where(lane_slot == q, block, block_of)
            sign_of = jnp.where(lane_slot == q, sign.astype(F32), sign_of)

    def pack(n, faces):
        fsend[n] = dot(pick[...], faces).astype(BF16).reshape(SLOTS, FACE_ROWS, LOADS)

    def send_faces(n):
        for w, move in enumerate(MOVES):
            span = pl.ds(w * CAP, CAP)
            remote(fsend.at[n, span], farr.at[n, span], fs.at[n], fr.at[n], around[-move])

    def arrived(n):
        return farr[n].reshape(SLOT_ROWS, LOADS)

    def remainder(value):
        return (value - value.astype(BF16).astype(F32)).astype(BF16)

    fetches[0].wait()
    vz[...] = out[...].astype(BF16)
    pack(LAM_HI, vz[0:FACE_TOTAL, :])
    low[...] = remainder(out[0:FACE_TOTAL, :])
    pl.semaphore_wait(barrier, len(MOVES) + NL - 1 + NXY - 1)
    send_faces(LAM_HI)

    own_slot = []
    own_off = [face_offset[f, s] for f in range(FACES)]
    for f in range(FACES):
        rank = jnp.int32(0)
        for g in range(f):
            rank = rank + jnp.where(own_off[g] == own_off[f], 1, 0)
        own_slot.append(own_off[f] * CAP + rank)
        sign = (2 * face_sign[f, s] - 1).astype(F32)
        place[f * FACE_ROWS : (f + 1) * FACE_ROWS, :] = jnp.where(wide == own_slot[f], sign, 0.0).astype(BF16)
    for q in range(SLOTS):
        face = jnp.int32(0)
        for f in range(FACES):
            face = face + jnp.where(own_slot[f] == q, f, 0)
        leave[q * FACE_ROWS : (q + 1) * FACE_ROWS, :] = ones_where(narrow == face)

    def cut_coarse():
        fetches[2].wait()
        cpad[...] = jnp.zeros(cpad.shape, F32)
        for b in range(NX):
            cpad[b * 8 : b * 8 + MODES, :] = cinv[b * MODES : (b + 1) * MODES, :]
        half = cinv.shape[1] // 2
        stack = jnp.concatenate(parts_of(cpad[...], 3), axis=0).astype(BF16)
        row = iota((half, LOADS), 0)
        col = iota((half, LOADS), 1)
        want = jnp.where((col & 7) < MODES, (col >> 3) * (NX * MODES) + (col & 7), -NX * MODES)
        for xd in range(NX):
            choose = ones_where(row == want + xd * MODES)
            for h in range(2):
                got = dot(stack[:, h * half : (h + 1) * half], choose)
                csend[xd * 2 + h] = got[0:32] + got[32:64] + got[64:96]
                yd = 2 * x + h
                mine = (yd == y) & (x == xd)

                @pl.when(mine)
                def _():
                    pltpu.make_async_copy(csend.at[xd * 2 + h], cmat.at[y], kr).start()

                @pl.when(jnp.logical_not(mine))
                def _():
                    remote(csend.at[xd * 2 + h], cmat.at[y], ks, kr, (yd * NL + l, xd))

    def residual(rows_from, rows_to):
        g_hi, g_lo = parts_of(grad[rows_from:rows_to, :], 2)
        m = modes_rows[:, rows_from:rows_to]
        a = dot(m, g_hi.astype(BF16))
        b = dot(m, g_lo.astype(BF16))
        return a[0:8] + a[8:16] + b[0:8]

    def row_of_ones(t):
        return ones_where(iota((LOADS, LOADS), 0) == t)

    def step(t):
        if t == 0:
            cut_coarse()
            fetches[1].wait()
            m_pad = jnp.concatenate([modes[...], jnp.zeros((2, ORDER), F32)], axis=0)
            m_hi, m_lo = parts_of(m_pad, 2)
            modes_rows[...] = jnp.concatenate([m_hi, m_lo], axis=0).astype(BF16)
            fetches[4].wait()
            wait_bytes(fr.at[LAM_HI], farr.at[LAM_HI])
            came = dot(place[...], arrived(LAM_HI))
        else:
            vz[...] = out[...].astype(BF16)
            came = dot(place[...], lam_far[...].astype(BF16))
        vz[0:FACE_TOTAL, :] = (vz[0:FACE_TOTAL, :].astype(F32) + came).astype(BF16)
        ybf[...] = dot(dual[0, 0:FACE_TOTAL, :], vz[...]).astype(BF16)
        bsend[t] = dot(leave[...], ybf[...]).astype(BF16).reshape(SLOTS, FACE_ROWS, LOADS)
        for w, move in enumerate(MOVES):
            span = pl.ds(w * CAP, CAP)
            remote(bsend.at[t, span], barr.at[t, span], bs.at[t], br.at[t], around[move])
        if t == 0:
            fetches[5].wait()
            for b in range(FACES):
                hit = (wide >= 0) & (block_of == b)
                spread[b * FACE_ROWS : (b + 1) * FACE_ROWS, :] = jnp.where(hit, sign_of, 0.0).astype(BF16)
        y_rest = dot(dual[0, FACE_TOTAL:, :], vz[...]).astype(BF16).astype(F32)
        grad[FACE_TOTAL:, :] = y_rest - loads[FACE_TOTAL:, :]
        e_rest = residual(FACE_TOTAL, ORDER)
        y_less = ybf[...].astype(F32) - loads[0:FACE_TOTAL, :]
        wait_bytes(br.at[t], barr.at[t])
        grad[0:FACE_TOTAL, :] = y_less + dot(spread[...], barr[t].reshape(SLOT_ROWS, LOADS))
        eline[t, l] = e_rest + residual(0, FACE_TOTAL)

        for device in line:
            remote(eline.at[t, l], eline.at[t, l], es.at[t], er.at[t], device)
        if t == 0:
            m_all = jnp.concatenate([m_hi, m_hi, m_lo, jnp.zeros((8, ORDER), F32)], axis=0).astype(BF16)
            modes_cols[...] = dot_t(m_all, ones_where(iota((32, 32), 0) == iota((32, 32), 1))).astype(BF16)
            fetches[3].wait()
            con = jnp.concatenate([contact[...].astype(F32), jnp.zeros((16 - STEPS, ORDER), F32)], axis=0).astype(BF16)
            columns[...] = dot_t(con, ones_where(iota((16, LOADS), 0) == iota((16, LOADS), 1))).astype(BF16)
            wait_bytes(kr, cmat)
        wait_bytes(er.at[t], eline.at[t, pl.ds(0, NL - 1)])
        product = jnp.dot(
            cmat[...].reshape(NXY * 8, LOADS), eline[t].reshape(NL * 8, LOADS),
            precision=lax.Precision.HIGHEST, preferred_element_type=F32,
        )
        part[t] = product.reshape(NXY, 8, LOADS)
        for q, device in plane:
            remote(part.at[t, q], cpl.at[t, me], cs.at[t], cr.at[t], device)
        cpl[t, me] = part[t, me]
        if t == 0:
            pack(LAM_LO, low[...])
            send_faces(LAM_LO)
            pack(CONTACT, columns[0:FACE_TOTAL, :])
            send_faces(CONTACT)
            for i in range(STEPS):
                floor[i] = jnp.where(dot(columns[...], row_of_ones(i)) > 0.5, 0.0, LOW)
        wait_bytes(cr.at[t], cpl.at[t, pl.ds(0, NXY - 1)])
        c_hi, c_lo = parts_of(jnp.sum(cpl[t], axis=0), 2)
        c_all = jnp.concatenate([c_hi, c_lo, c_hi, jnp.zeros((8, LOADS), F32)], axis=0).astype(BF16)

        def correct(rows_from, rows_to):
            value = grad[rows_from:rows_to, :] - dot(modes_cols[rows_from:rows_to, :], c_all)
            dirn[rows_from:rows_to, :] = value
            vz[rows_from:rows_to, :] = value.astype(BF16)

        correct(0, FACE_TOTAL)
        pack(DIR_HI + t, vz[0:FACE_TOTAL, :])
        send_faces(DIR_HI + t)
        correct(FACE_TOTAL, ORDER)
        slope = jnp.sum(grad[...] * dirn[...], axis=0, keepdims=True)
        image[...] = dot(dual[0, :, FACE_TOTAL:], vz[FACE_TOTAL:, :])

        wait_bytes(fr.at[DIR_HI + t], farr.at[DIR_HI + t])
        z = vz[0:FACE_TOTAL, :].astype(F32) + dot(place[...], arrived(DIR_HI + t))
        zf[...] = z
        whole = image[...] + dot(dual[0, :, 0:FACE_TOTAL], z.astype(BF16))
        curv = jnp.sum(zf[...] * whole[0:FACE_TOTAL], axis=0, keepdims=True)
        curv = curv + jnp.sum(dirn[FACE_TOTAL:, :] * whole[FACE_TOTAL:], axis=0, keepdims=True)
        arl[t, l] = jnp.concatenate([slope, curv], axis=0)
        for device in line:
            remote(arl.at[t, l], arl.at[t, l], als.at[t], alr.at[t], device)
        last = t == STEPS - 1
        if not last:
            pack(DIR_LO + t, remainder(dirn[0:FACE_TOTAL, :]))
            send_faces(DIR_LO + t)
        wait_bytes(alr.at[t], arl.at[t, pl.ds(0, NL - 1)])
        arp[t, me] = jnp.sum(arl[t], axis=0)
        for _, device in plane:
            remote(arp.at[t, me], arp.at[t, me], aps.at[t], apr.at[t], device)

        if t == 0:
            wait_bytes(fr.at[LAM_LO], farr.at[LAM_LO])
            wait_bytes(fr.at[CONTACT], farr.at[CONTACT])
            lam_far[...] = arrived(LAM_HI).astype(F32) + arrived(LAM_LO).astype(F32)
            for i in range(STEPS - 1):
                floor_far[i] = jnp.where(dot(arrived(CONTACT), row_of_ones(i)) > 0.5, 0.0, LOW)
        if not last:
            wait_bytes(fr.at[DIR_LO + t], farr.at[DIR_LO + t])
        wait_bytes(apr.at[t], arp.at[t, pl.ds(0, NXY - 1)])
        total = jnp.sum(arp[t], axis=0)
        alpha = total[0:1] / total[1:2]
        if not last:
            dirn_far = arrived(DIR_HI + t).astype(F32) + arrived(DIR_LO + t).astype(F32)
            lam_far[...] = jnp.maximum(lam_far[...] - alpha * dirn_far, floor_far[t])
        out[...] = jnp.maximum(out[...] - alpha * dirn[...], floor[t])

    for t in range(STEPS):
        step(t)

    for n in range(MESSAGES):
        wait_bytes(fs.at[n], fsend.at[n])
    for t in range(STEPS):
        wait_bytes(bs.at[t], bsend.at[t])
        wait_bytes(es.at[t], eline.at[t, pl.ds(0, NL - 1)])
        wait_bytes(cs.at[t], part.at[t, pl.ds(0, NXY - 1)])
        wait_bytes(als.at[t], arl.at[t, pl.ds(0, NL - 1)])
        wait_bytes(aps.at[t], arp.at[t, pl.ds(0, NXY - 1)])
    own_cut = x == y // 2

    @pl.when(own_cut)
    def _():
        wait_bytes(ks, csend.at[pl.ds(0, 7)])

    @pl.when(jnp.logical_not(own_cut))
    def _():
        wait_bytes(ks, csend)


def on_device(lam_start, loads, dual_ops, modes, coarse_inverse, face_offset, face_block, face_sign, contact):
    tables = [face[:, 0, :].T for face in (face_offset, face_block, face_sign)]
    whole = pl.BlockSpec(memory_space=pl.ANY)
    smem = pl.BlockSpec(memory_space=pltpu.SMEM)
    vmem, dma = pltpu.VMEM, pltpu.SemaphoreType.DMA
    return pl.pallas_call(
        kernel,
        name="dual_steps",
        out_shape=jax.ShapeDtypeStruct(lam_start.shape, F32),
        in_specs=[smem] * 3 + [whole] * 6,
        out_specs=pl.BlockSpec(memory_space=pltpu.VMEM),
        scratch_shapes=[
            vmem(loads.shape, F32),
            vmem(dual_ops.shape, BF16),
            vmem(modes.shape, F32),
            vmem(coarse_inverse.shape, F32),
            vmem(contact.shape, jnp.int32),
            vmem((FACE_TOTAL, SLOT_ROWS), BF16),
            vmem((SLOT_ROWS, FACE_TOTAL), BF16),
            vmem((SLOT_ROWS, FACE_TOTAL), BF16),
            vmem((FACE_TOTAL, SLOT_ROWS), BF16),
            vmem((ORDER, LOADS), BF16),
            vmem((FACE_TOTAL, LOADS), BF16),
            vmem((FACE_TOTAL, LOADS), BF16),
            vmem((FACE_TOTAL, LOADS), F32),
            vmem((ORDER, LOADS), F32),
            vmem((ORDER, LOADS), F32),
            vmem((ORDER, LOADS), F32),
            vmem((SLOT_ROWS, LOADS), F32),
            vmem((16, ORDER), BF16),
            vmem((ORDER, 32), BF16),
            vmem((ORDER, LOADS), BF16),
            vmem((STEPS, ORDER, LOADS), F32),
            vmem((STEPS - 1, SLOT_ROWS, LOADS), F32),
            vmem((MESSAGES, SLOTS, FACE_ROWS, LOADS), BF16),
            vmem((MESSAGES, SLOTS, FACE_ROWS, LOADS), BF16),
            vmem((STEPS, SLOTS, FACE_ROWS, LOADS), BF16),
            vmem((STEPS, SLOTS, FACE_ROWS, LOADS), BF16),
            vmem((STEPS, NL, 8, LOADS), F32),
            vmem((STEPS, NXY, 8, LOADS), F32),
            vmem((STEPS, NXY, 8, LOADS), F32),
            vmem((STEPS, NL, 2, LOADS), F32),
            vmem((STEPS, NXY, 2, LOADS), F32),
            vmem((8, 32, LOADS), F32),
            vmem((8, 32, LOADS), F32),
            vmem((32, coarse_inverse.shape[1]), F32),
            dma((6,)),
            dma((MESSAGES,)),
            dma((MESSAGES,)),
        ]
        + [dma((STEPS,))] * 10
        + [dma, dma],
        compiler_params=pltpu.CompilerParams(collective_id=1, has_side_effects=True),
    )(*tables, lam_start, loads, dual_ops, modes, coarse_inverse, contact)


def solution(mesh):
    both = ("sub", "grp")
    placed = (
        P(both, None),
        P(both, None),
        P(both, None, None),
        P(None, both),
        P("sub", "grp"),
        P(None, "grp", None),
        P(None, "grp", None),
        P(None, "grp", None),
        P(None, both),
    )
    return jax.shard_map(on_device, mesh=mesh, in_specs=placed, out_specs=P(both, None), check_vma=False)
```
